32 devices in a mesh: dp: 8 (over z, x), ctx: 4 (over y, core).
Axes of the slice: x: 2, y: 2, z: 4, core: 2. Of those that a mesh axis runs over, the one named last changes fastest.
Arguments:
- features: bfloat16 [4096, 4096], P(('dp', 'ctx')), may hold values from -6 to 6
- gate_in: bfloat16 [4096, 4096], P(('dp', 'ctx')), may hold values from -6 to 6
- gate_out: bfloat16 [4096, 4096], P(('dp', 'ctx')), may hold values from -6 to 6
- value_weight: bfloat16 [4096, 4096], P('dp', 'ctx'), may hold values from -0.09375 to 0.09375
- short_taps: float32 [3, 7, 4096], replicated, may hold values from -2 to 2
- medium_taps: bfloat16 [128, 256], replicated, may hold values from -0.5 to 0.5
- cotangent: bfloat16 [4096, 4096], P(('dp', 'ctx')), may hold values from -6 to 6
Outputs:
- layer_out: bfloat16 [4096, 4096], P(('dp', 'ctx'))
- grad_features: bfloat16 [4096, 4096], P(('dp', 'ctx'))
- grad_gate_in: bfloat16 [4096, 4096], P(('dp', 'ctx'))
- grad_gate_out: bfloat16 [4096, 4096], P(('dp', 'ctx'))
- grad_weight: bfloat16 [4096, 4096], P('dp', 'ctx')
- grad_short: float32 [3, 7, 4096], P(None, None, 'ctx')
- grad_medium: float32 [128, 256], P(None, 'ctx')
The draws below stay inside these ranges and needn't reach their ends.
All inputs are finite; a program needn't handle non-finite values.
Results may differ from the reference program's by a relative error of at most 0.025.
Values may be sent and summed in bfloat16 or wider, within the bound.
A program may use at most 256 MiB of HBM per device.

```python
import math
import jax
import jax.numpy as jnp
from jax import lax

D = 4096
GROUP_WIDTH = 16
GROUPS = 256
KS = 7
FILT = 128
LEN = 512
WINDOWS = 8
TOKENS = 4096
N_CTX = 4


def strengthened(array, rng, source, target, parts, factor):
    owner, partner = [(jnp.arange(array.shape[dim]) // (array.shape[dim] // parts)).reshape([-1 if axis == dim else 1 for axis in range(array.ndim)]) for dim in (source, target)]
    chosen = jax.random.permutation(rng, parts)[partner]
    strong = (owner == chosen) | (owner == (partner + parts // 2) % parts)
    return jnp.where(strong, factor * array, array)


def shard_levels(key, dims, split, smallest, largest):
    factor_of = 1.0
    for axis_at, parts in split:
        heights = jax.random.uniform(jax.random.fold_in(jax.random.fold_in(key, 6), axis_at), (parts,), jnp.float32, smallest / len(split), largest / len(split))
        factor_of = factor_of * jnp.repeat(jnp.exp(heights), dims[axis_at] // parts).reshape((-1,) + (1,) * (len(dims) - 1 - axis_at))
    return factor_of


def bell_draw(key, shape, scale, bound, cuts=(), kind=jnp.bfloat16):
    drawn = jax.random.normal(key, shape, jnp.float32) * scale
    if len(cuts) > 0:
        drawn = shard_levels(key, shape, cuts, -0.22, 0.18) * drawn
    return jnp.clip(drawn, min=-bound, max=bound).astype(kind)


def bell_draw_with(stream_key, dims, spread, bound, shards, heavy, held_as=jnp.bfloat16):
    result = spread * jax.random.normal(stream_key, dims, jnp.float32)
    if shards:
        result = result * shard_levels(stream_key, dims, shards, -0.22, 0.18)
    return jnp.clip(strengthened(result, jax.random.fold_in(stream_key, 3), *heavy), -bound, bound).astype(held_as)


def setup_inputs(seed: int = 0) -> dict:
    arg_keys = jax.random.split(jax.random.key(seed), 8)
    return {
        "features": bell_draw_with(arg_keys[0], (TOKENS, D), 1.0, 6.0, ((0, 32),), (0, 1, 32, 2.75)),
        "gate_in": bell_draw(arg_keys[1], (TOKENS, D), 1.0, 6.0, ((0, 32),)),
        "gate_out": bell_draw(arg_keys[2], (TOKENS, D), 1.0, 6.0, ((0, 32),)),
        "value_weight": bell_draw(arg_keys[3], (D, D), D ** -0.5, 0.09375, ((0, 8), (1, 4))),
        "short_taps": bell_draw(arg_keys[4], (3, KS, D), KS ** -0.5, 2.0, (), jnp.float32),
        "medium_taps": bell_draw(arg_keys[5], (FILT, GROUPS), FILT ** -0.5, 0.5),
        "cotangent": bell_draw(arg_keys[6], (TOKENS, D), 1.0, 6.0, ((0, 32),)),
    }


def causal_conv(stream, conv_taps, prior_rows):
    conv_edge = conv_taps.shape[0] - 1
    row_count = stream.shape[0]
    extended = jnp.concatenate([prior_rows, stream], axis=0)
    running = conv_taps[0] * extended[conv_edge:conv_edge + row_count]
    for shift_back in range(1, conv_edge + 1):
        running = running + conv_taps[shift_back] * extended[conv_edge - shift_back:conv_edge - shift_back + row_count]
    return running

def conv_back(gradient, conv_taps, later_rows):
    conv_edge = conv_taps.shape[0] - 1
    row_count = gradient.shape[0]
    extended = jnp.concatenate([gradient, later_rows], axis=0)
    running = conv_taps[0] * extended[:row_count]
    for ahead in range(1, conv_edge + 1):
        running = running + conv_taps[ahead] * extended[ahead:ahead + row_count]
    return running

def conv_taps_grad(gradient, stream, prior_rows):
    conv_edge = prior_rows.shape[0]
    row_count = stream.shape[0]
    extended = jnp.concatenate([prior_rows, stream], axis=0)
    return jnp.stack([lax.optimization_barrier(jnp.sum(gradient * extended[conv_edge - shift_back:conv_edge - shift_back + row_count], axis=0)) for shift_back in range(conv_edge + 1)])

def toeplitz_table(medium):
    filter_span, group_count = medium.shape
    padded = jnp.concatenate([jnp.zeros((1, group_count), medium.dtype), medium[::-1], jnp.zeros((filter_span, group_count), medium.dtype)], axis=0)
    tiled = jnp.tile(padded.T, (1, filter_span))
    return tiled[:, :2 * filter_span * filter_span].reshape(group_count, filter_span, 2 * filter_span)

def fold_table(grad_table):
    group_count, filter_span, double_span = grad_table.shape
    flat = grad_table.reshape(group_count, filter_span * double_span)
    flat = jnp.concatenate([flat, jnp.zeros((group_count, filter_span), grad_table.dtype)], axis=1)
    summed = lax.optimization_barrier(jnp.sum(flat.reshape(group_count, filter_span, double_span + 1), axis=1))
    return summed[:, 1:filter_span + 1][:, ::-1].T

def apply_toeplitz(toeplitz, before, product):
    group_count, filter_span = (toeplitz.shape[0], toeplitz.shape[1])
    row_count, channels = product.shape
    block_shape = (row_count // filter_span, filter_span, group_count, channels // group_count)
    extended = jnp.concatenate([before, product], axis=0)
    lower_half = extended[:row_count].reshape(block_shape)
    upper_half = extended[filter_span:].reshape(block_shape)
    window = jnp.concatenate([lower_half, upper_half], axis=1)
    filtered = jnp.einsum('gij,bjgs->bigs', toeplitz.astype(jnp.float32), window.astype(jnp.float32))
    return (filtered.reshape(row_count, channels), window)

def toeplitz_back(toeplitz, medium, grad_filtered, later_rows, window):
    group_count, filter_span = (toeplitz.shape[0], toeplitz.shape[1])
    row_count, channels = grad_filtered.shape
    block_shape = (row_count // filter_span, filter_span, group_count, channels // group_count)
    current = grad_filtered.reshape(block_shape).astype(jnp.float32)
    following = jnp.concatenate([grad_filtered[filter_span:], later_rows], axis=0).reshape(block_shape).astype(jnp.float32)
    table = toeplitz.astype(jnp.float32)
    grad_product = jnp.einsum('gij,bigs->bjgs', table[:, :, filter_span:], current) + jnp.einsum('gij,bigs->bjgs', table[:, :, :filter_span], following)
    grad_table = jnp.einsum('bigs,bjgs->gij', current, window.astype(jnp.float32))
    return (grad_product.reshape(row_count, channels), fold_table(grad_table))

def reference(features, gate_in, gate_out, value_weight, short_taps, medium_taps, cotangent):
    row_scale = 1.0 / math.sqrt(TOKENS)
    group_scale = 1.0 / math.sqrt(TOKENS * GROUP_WIDTH)
    toeplitz = toeplitz_table(medium_taps)
    zero_rim = jnp.zeros((KS - 1, D), jnp.bfloat16)
    zero_span = jnp.zeros((FILT, D), jnp.bfloat16)
    zero_after = jnp.zeros((KS - 1, D), jnp.float32)
    weight_blocks = value_weight.reshape(D, N_CTX, D // N_CTX).astype(jnp.float32)

    def one_window(state_sums, pieces):
        weight_sum, short_sum, medium_sum = state_sums
        window_features, window_in, window_out, window_cot = pieces
        values = jnp.dot(window_features, value_weight, preferred_element_type=jnp.float32).astype(jnp.bfloat16)
        streams = (window_in, window_out, values)
        convs = [causal_conv(streams[index], short_taps[index], zero_rim) for index in range(3)]
        product = (convs[0] * convs[2]).astype(jnp.bfloat16)
        filtered, window = apply_toeplitz(toeplitz, zero_span, product)
        layer_out = (convs[1] * filtered).astype(jnp.bfloat16)
        grad_filtered = (window_cot * convs[1]).astype(jnp.bfloat16)
        grad_product, medium_grad = toeplitz_back(toeplitz, medium_taps, grad_filtered, zero_span, window)
        grad_convs = (grad_product * convs[2], window_cot * filtered, grad_product * convs[0])
        grad_streams = [conv_back(grad_convs[index], short_taps[index], zero_after) for index in range(3)]
        short_grad = jnp.stack([conv_taps_grad(grad_convs[index], streams[index], zero_rim) for index in range(3)])
        grad_values = grad_streams[2].astype(jnp.bfloat16)
        window_term = lax.dot_general(window_features, grad_values, (((0,), (0,)), ((), ())), preferred_element_type=jnp.float32) * row_scale
        window_term = lax.optimization_barrier(window_term.astype(jnp.bfloat16)).astype(jnp.float32)
        value_blocks = grad_values.reshape(LEN, N_CTX, D // N_CTX).astype(jnp.float32)
        block_terms = jnp.einsum('tjc,djc->jtd', value_blocks, weight_blocks)
        block_terms = lax.optimization_barrier(block_terms.astype(jnp.bfloat16)).astype(jnp.float32)
        grad_features = lax.optimization_barrier(jnp.sum(block_terms, axis=0)).astype(jnp.bfloat16)
        new_sums = (weight_sum + window_term, short_sum + short_grad * row_scale, medium_sum + medium_grad * group_scale)
        return (new_sums, (layer_out, grad_features, grad_streams[0].astype(jnp.bfloat16), grad_streams[1].astype(jnp.bfloat16)))
    start_sums = (jnp.zeros((D, D), jnp.float32), jnp.zeros((3, KS, D), jnp.float32), jnp.zeros((FILT, GROUPS), jnp.float32))
    stacked = (features.reshape(WINDOWS, LEN, D), gate_in.reshape(WINDOWS, LEN, D), gate_out.reshape(WINDOWS, LEN, D), cotangent.reshape(WINDOWS, LEN, D))
    final_sums, outputs = lax.scan(one_window, start_sums, stacked)
    layer_out, grad_features, grad_gate_in, grad_gate_out = [piece.reshape(TOKENS, D) for piece in outputs]
    return (layer_out, grad_features, grad_gate_in, grad_gate_out, final_sums[0].astype(jnp.bfloat16), final_sums[1], final_sums[2])
```

```python
import functools
import math

import jax
import jax.numpy as jnp
from jax import lax
from jax.experimental import pallas as pl
from jax.experimental.pallas import tpu as pltpu
from jax.sharding import PartitionSpec as P

MESH = pl.DeviceIdType.MESH
ANY = pl.BlockSpec(memory_space=pl.ANY)
LANES = 128
CHUNK = 64
VMEM = pl.BlockSpec(memory_space=pltpu.VMEM)
F32, BF16 = jnp.float32, jnp.bfloat16


def greet(dp, ctx):
    me_dp, me_ctx = lax.axis_index("dp"), lax.axis_index("ctx")
    barrier = pltpu.get_barrier_semaphore()
    for step in range(1, dp):
        pl.semaphore_signal(
            barrier, inc=1, device_id=(lax.rem(me_dp + step, dp), me_ctx), device_id_type=MESH
        )
    for step in range(1, ctx):
        pl.semaphore_signal(
            barrier, inc=1, device_id=(me_dp, lax.rem(me_ctx + step, ctx)), device_id_type=MESH
        )
    pl.semaphore_wait(barrier, dp + ctx - 2)


def send(src, dst, send_sem, recv_sem, device):
    return pltpu.make_async_remote_copy(
        src_ref=src,
        dst_ref=dst,
        send_sem=send_sem,
        recv_sem=recv_sem,
        device_id=device,
        device_id_type=MESH,
    )


def spread(source, target, groups, span):
    offset = lax.broadcasted_iota(jnp.int32, (8, 2 * span), 0)
    for group in range(groups):
        rows = jnp.broadcast_to(source[group : group + 1], (8, 2 * span))
        for bit in (1, 2, 4):
            rows = jnp.where((offset & bit) != 0, pltpu.roll(rows, bit, 1), rows)
        height = 8
        while height < span:
            rows = jnp.concatenate([rows, pltpu.roll(rows, height, 1)], axis=0)
            height *= 2
        target[group * span : (group + 1) * span] = rows.astype(BF16)


def filter_back(table, source, target, length, groups, span, owner):
    for base in range(0, length, span):
        chosen = None
        for group in range(groups):
            out = jnp.dot(
                table[group * span : (group + 1) * span], source[base : base + 2 * span],
                preferred_element_type=F32,
            )
            chosen = out if chosen is None else jnp.where(owner == group, out, chosen)
        target[base : base + span] = chosen


def ahead_conv(taps, index, stream, base, edge):
    running = taps[index, 0:1] * stream[8 + base : 8 + base + CHUNK]
    for shift in range(1, edge):
        start = 8 + base - shift
        running = running + taps[index, shift : shift + 1] * stream[start : start + CHUNK]
    return running


class Copies:
    def __init__(self):
        self.count = 0

    def take(self, *shape):
        base, self.count = self.count, self.count + math.prod(shape)
        strides = [math.prod(shape[at + 1 :]) for at in range(len(shape))]
        return lambda *at: base + sum(i * s for i, s in zip(at, strides))


class Plan:
    def __init__(self, dp, ctx, chunks):
        self.dp, self.ctx, self.chunks = dp, ctx, chunks
        self.line, self.tall = dp // 4, ctx // 2
        line, tall = self.line, self.tall
        far = max(line - 1, 1)
        away = max(tall - 1, 1)
        remote = Copies()
        self.w_x = remote.take(chunks)
        self.w_far = remote.take(far, chunks)
        self.w_relay = remote.take(far, chunks)
        self.f_z = remote.take(line)
        self.f_y = remote.take(2, away)
        self.f_core = remote.take(2, tall)
        self.gates = remote.take(chunks, 3, ctx)
        self.grad = remote.take(chunks)
        self.part = remote.take(chunks)
        self.g_x = remote.take(chunks, line)
        self.g_far = remote.take(chunks, far)
        self.t_core = remote.take(2, tall)
        self.t_y = remote.take(2, away)
        self.t_z = remote.take(line)
        self.outs = remote.take(chunks, 3, ctx)
        self.small = remote.take(chunks, dp)
        self.remote = remote.count
        local = Copies()
        self.l_weight = local.take(1)
        self.l_features = local.take(line)
        self.l_gates = local.take(chunks, 3)
        self.l_outs = local.take(chunks, 3)
        self.l_terms = local.take(line)
        self.l_result = local.take(1)
        self.local = local.count


def group_rows(step, groups):
    return pl.ds(pl.multiple_of(step * groups, groups), groups)


def first_stage(group_width, gate_in, gate_out, cot, taps, behind, grad_values, kept, work):
    conv_in, conv_out, grad_filtered, grad_product = kept
    streams, grads, _, _, back = work
    length, edge, span = gate_in.shape[0], taps.shape[1], back.shape[1] // 2
    groups = LANES // group_width
    streams[0, 8:] = gate_in[...].astype(F32)
    streams[1, 8:] = gate_out[...].astype(F32)
    grad_filtered[length:] = jnp.zeros((span, LANES), BF16)
    spread(behind, back, groups, span)
    for base in range(0, length, CHUNK):
        part = slice(base, base + CHUNK)
        conv_in[part] = ahead_conv(taps, 0, streams.at[0], base, edge)
        conv = ahead_conv(taps, 1, streams.at[1], base, edge)
        conv_out[part] = conv
        grad_filtered[part] = (cot[part].astype(F32) * conv).astype(BF16)
    owner = lax.broadcasted_iota(jnp.int32, (span, LANES), 1) // group_width
    filter_back(back, grad_filtered, grad_product, length, groups, span, owner)
    grads[2, :length] = grad_product[...] * conv_in[...]
    for base in range(0, length, CHUNK):
        running = taps[2, 0:1] * grads[2, base : base + CHUNK]
        for shift in range(1, edge):
            start = base + shift
            running = running + taps[2, shift : shift + 1] * grads[2, start : start + CHUNK]
        grad_values[base : base + CHUNK] = running.astype(BF16)


def second_stage(
    group_width, gate_in, gate_out, cot, near, other, taps, ahead, layer, grad_in, grad_out, small,
    kept, work,
):
    conv_in, conv_out, grad_filtered, grad_product = kept
    streams, grads, product, filtered, table = work
    length, edge, span = gate_in.shape[0], taps.shape[1], table.shape[1] // 2
    groups = LANES // group_width
    streams[0, 8:] = gate_in[...].astype(F32)
    streams[1, 8:] = gate_out[...].astype(F32)
    streams[2, 8:] = (near[...] + other[...].astype(F32)).astype(BF16).astype(F32)
    spread(ahead, table, groups, span)
    for base in range(0, length, CHUNK):
        part = slice(base, base + CHUNK)
        conv = ahead_conv(taps, 2, streams.at[2], base, edge)
        front = conv_in[part]
        gradient = grad_product[part]
        product[span + base : span + base + CHUNK] = (front * conv).astype(BF16)
        grads[0, part] = gradient * conv
        grads[2, part] = gradient * front
    owner = lax.broadcasted_iota(jnp.int32, (span, LANES), 1) // group_width
    filter_back(table, product, filtered, length, groups, span, owner)
    offset = lax.broadcasted_iota(jnp.int32, (8, 2 * span), 0)
    for group in range(groups):
        total = None
        for base in range(0, length, span):
            current = grad_filtered[base : base + span].astype(F32)
            current = jnp.where(owner == group, current, 0.0).astype(BF16)
            term = lax.dot_general(
                current, product[base : base + 2 * span], (((1,), (1,)), ((), ())),
                preferred_element_type=F32,
            )
            total = term if total is None else total + term
        height = span // 2
        while height >= 8:
            total = total[:height] + pltpu.roll(total[height:], 2 * span - height, 1)
            height //= 2
        for bit in (1, 2, 4):
            total = jnp.where((offset & bit) != 0, pltpu.roll(total, 2 * span - bit, 1), total)
        total = pltpu.roll(total, 2 * span - 1, 1)
        small[24 + group : 25 + group] = jnp.sum(total, axis=0, keepdims=True)[:, :span]
    for base in range(0, length, CHUNK):
        part = slice(base, base + CHUNK)
        held = filtered[part]
        layer[part] = (conv_out[part] * held).astype(BF16)
        grads[1, part] = cot[part].astype(F32) * held
    outs = (grad_in, grad_out, None)
    for index in range(3):
        tap_sums = [jnp.zeros((8, LANES), F32) for _ in range(edge)]
        for base in range(0, length, CHUNK):
            stream = streams[index, 8 + base : 8 + base + CHUNK]
            running = None
            for shift in range(edge):
                gradient = grads[index, base + shift : base + shift + CHUNK]
                if index < 2:
                    term = taps[index, shift : shift + 1] * gradient
                    running = term if running is None else running + term
                tap_sums[shift] = tap_sums[shift] + jnp.sum(
                    (gradient * stream).reshape(CHUNK // 8, 8, LANES), axis=0
                )
            if index < 2:
                outs[index][base : base + CHUNK] = running.astype(BF16)
        for shift in range(edge):
            small[8 * index + shift : 8 * index + shift + 1] = jnp.sum(
                tap_sums[shift], axis=0, keepdims=True
            )


def fused_kernel(
    plan, group_width, row_scale, group_scale,
    features, gate_in, gate_out, cot, weight, taps, ahead, behind,
    weight_out, features_out, layer_out, first_out, second_out, short_out, medium_out,
    window, full, blocks, grads_in, near, part_send, part_recv,
    terms, terms_core, terms_y, weight_terms, weight_x, weight_far, sends, small,
    small_send, small_recv, result, conv_in, conv_out, grad_filtered, grad_product,
    streams, grads, product, filtered, table,
    send_sem, recv_sem, local_sem,
):
    dp, ctx, chunks, line, tall = plan.dp, plan.ctx, plan.chunks, plan.line, plan.tall
    me_dp, me_ctx = lax.axis_index("dp"), lax.axis_index("ctx")
    x, b, h = lax.rem(me_dp, 2), lax.rem(me_dp // 2, 2), me_dp // 4
    core = lax.rem(me_ctx, 2)
    y = me_ctx // 2
    x_peer = (me_dp + 1 - 2 * x, me_ctx)
    z_peer = (me_dp + 2 - 4 * b, me_ctx)
    mate = (me_dp, me_ctx + 1 - 2 * core)
    rows, channels = features.shape
    depth, cols = weight.shape
    length, half, wide = rows * ctx, 2 * line * depth, blocks.shape[3]
    per = wide // LANES
    groups = LANES // group_width

    def times(index, size):
        return pl.ds(pl.multiple_of(index * size, size), size)

    def far_dev(step):
        return (lax.rem(h + step, line) * 4 + b * 2 + x, me_ctx)

    def came_h(step):
        return lax.rem(h + line - step, line)

    def up(step):
        return (me_dp, 2 * lax.rem(y + step, tall) + core)

    def came_y(step):
        return lax.rem(y + tall - step, tall)

    def go(src, dst, index, device):
        return send(src, dst, send_sem.at[index], recv_sem.at[index], device)

    piece = depth // chunks

    def weight_rows(hh, xx, p):
        return full.at[pl.ds(pl.multiple_of((hh * 2 + xx) * depth + p * piece, piece), piece)]

    def w_x(p):
        return go(weight.at[times(p, piece)], weight_rows(h, x, p), plan.w_x(p), x_peer)

    def w_far(s, p):
        return go(
            weight.at[times(p, piece)], weight_rows(h, x, p), plan.w_far(s - 1, p), far_dev(s)
        )

    def w_relay(s, p):
        spot = weight_rows(came_h(s), x, p)
        return go(spot, spot, plan.w_relay(s - 1, p), x_peer)

    own_weight = pltpu.make_async_copy(
        weight, full.at[times(h * 2 + x, depth)], local_sem.at[plan.l_weight(0)]
    )

    def window_rows(w, quarter):
        return window.at[pl.ds(pl.multiple_of(w * length + quarter * rows, rows), rows)]

    def half_cols(g, side):
        return times(g * 2 + side, 2 * depth)

    def f_local(g):
        return pltpu.make_async_copy(
            features.at[:, half_cols(g, b)],
            window_rows(0, me_ctx).at[:, g * 2 * depth : (g + 1) * 2 * depth],
            local_sem.at[plan.l_features(g)],
        )

    def f_z(g):
        return go(
            features.at[:, half_cols(g, 1 - b)],
            window_rows(1, me_ctx).at[:, g * 2 * depth : (g + 1) * 2 * depth],
            plan.f_z(g), z_peer,
        )

    def f_y(w, s):
        spot = window_rows(w, me_ctx)
        return go(spot, spot, plan.f_y(w, s - 1), up(s))

    def f_core(w, s):
        spot = window_rows(w, 2 * came_y(s) + core)
        return go(spot, spot, plan.f_core(w, s), mate)

    stream_refs = (gate_in, gate_out, cot)

    def gates(c, which, s):
        peer = lax.rem(me_ctx + s, ctx)
        spot = pl.ds(pl.multiple_of(peer * cols + c * wide, wide), wide)
        return go(
            stream_refs[which].at[:, spot], blocks.at[which, c, times(me_ctx, rows)],
            plan.gates(c, which, s), (me_dp, peer),
        )

    def gates_local(c, which):
        spot = pl.ds(pl.multiple_of(me_ctx * cols + c * wide, wide), wide)
        return pltpu.make_async_copy(
            stream_refs[which].at[:, spot], blocks.at[which, c, times(me_ctx, rows)],
            local_sem.at[plan.l_gates(c, which)],
        )

    def gates_start(c):
        for which in range(3):
            for s in range(1, ctx):
                gates(c, which, s).start()
            gates_local(c, which).start()

    def gates_wait(c):
        for which in range(3):
            for s in range(1, ctx):
                gates(c, which, s).wait_recv()
            gates_local(c, which).wait()

    def grad_copy(c):
        return go(grads_in.at[c, :length], grads_in.at[c, length:], plan.grad(c), z_peer)

    def part_copy(c):
        return go(part_send.at[c], part_recv.at[c], plan.part(c), z_peer)

    def g_x(c, hh):
        return go(
            weight_terms.at[c, times(hh * 2 + 1 - x, depth)], weight_x.at[c, hh],
            plan.g_x(c, hh), x_peer,
        )

    def g_far(c, s):
        return go(
            weight_terms.at[c, times(lax.rem(h + s, line) * 2 + x, depth)],
            weight_far.at[c, s - 1], plan.g_far(c, s - 1), far_dev(s),
        )

    def term_rows(w, quarter):
        return pl.ds(pl.multiple_of(w * length + quarter * rows, rows), rows)

    def t_core(w, i):
        return go(
            terms.at[term_rows(w, 2 * i + 1 - core)], terms_core.at[w, i], plan.t_core(w, i), mate
        )

    def t_y(w, s):
        return go(
            terms.at[term_rows(w, 2 * lax.rem(y + s, tall) + core)], terms_y.at[w, s - 1],
            plan.t_y(w, s - 1), up(s),
        )

    def t_z(g):
        return go(
            result.at[1, :, g * 2 * depth : (g + 1) * 2 * depth],
            features_out.at[:, half_cols(g, b)], plan.t_z(g), z_peer,
        )

    def t_local(g):
        return pltpu.make_async_copy(
            result.at[0, :, g * 2 * depth : (g + 1) * 2 * depth],
            features_out.at[:, half_cols(g, b)], local_sem.at[plan.l_terms(g)],
        )

    out_refs = (layer_out, first_out, second_out)

    def outs(c, which, s):
        peer = lax.rem(me_ctx + s, ctx)
        spot = pl.ds(pl.multiple_of(me_ctx * cols + c * wide, wide), wide)
        return go(
            sends.at[which, c, times(peer, rows)], out_refs[which].at[:, spot],
            plan.outs(c, which, s), (me_dp, peer),
        )

    def outs_local(c, which):
        spot = pl.ds(pl.multiple_of(me_ctx * cols + c * wide, wide), wide)
        return pltpu.make_async_copy(
            sends.at[which, c, times(me_ctx, rows)], out_refs[which].at[:, spot],
            local_sem.at[plan.l_outs(c, which)],
        )

    def small_copy(c, s):
        return go(
            small_send.at[c], small_recv.at[s - 1, c], plan.small(c, s),
            (lax.rem(me_dp + s, dp), me_ctx),
        )

    def repeat(count, body):
        def step(at, carry):
            body(at)
            return carry

        lax.fori_loop(0, count, step, 0)

    def lane_refs(c, u):
        lanes = pl.ds(pl.multiple_of(u * LANES, LANES), LANES)
        place = c * per + u
        tap_lanes = pl.ds(pl.multiple_of(place * LANES, LANES), LANES)
        kept = (
            conv_in.at[place], conv_out.at[place], grad_filtered.at[place], grad_product.at[place]
        )
        inputs = [blocks.at[which, c, :, lanes] for which in range(3)]
        return lanes, place, taps.at[:, :, tap_lanes], kept, inputs

    work = (streams, grads, product, filtered, table)

    def stage_one(c):
        def one(u):
            lanes, place, tap, kept, inputs = lane_refs(c, u)
            first_stage(
                group_width, *inputs, tap, behind.at[group_rows(place, groups)],
                grads_in.at[c, :length, lanes], kept, work,
            )

        repeat(per, one)

    def stage_two(c):
        def one(u):
            lanes, place, tap, kept, inputs = lane_refs(c, u)
            second_stage(
                group_width, *inputs, near.at[c, :, lanes], part_recv.at[c, :, lanes], tap,
                ahead.at[group_rows(place, groups)], sends.at[0, c, :, lanes],
                sends.at[1, c, :, lanes], sends.at[2, c, :, lanes], small.at[:, lanes], kept, work,
            )

        repeat(per, one)
        small_send[c, :24] = (small[:24] * row_scale).astype(BF16)
        small_send[c, 24:] = (small[24:] * group_scale).astype(BF16)
        for which in range(3):
            for s in range(1, ctx):
                outs(c, which, s).start()
            outs_local(c, which).start()
        for s in range(1, dp):
            small_copy(c, s).start()

    def weight_term(c):
        grad_copy(c).wait_recv()

        def one(i):
            side = jnp.where(i < line, 1 - x, x)
            spot = times(lax.rem(i, line) * 2 + side, depth)
            weight_terms[c, spot] = (
                lax.dot_general(
                    window[:, spot], grads_in[c], (((0,), (0,)), ((), ())),
                    preferred_element_type=F32,
                )
                * row_scale
            ).astype(BF16)

        repeat(line, one)
        for hh in range(line):
            g_x(c, hh).start()
        repeat(line, lambda i: one(i + line))

    def weight_pass(c):
        for hh in range(line):
            g_x(c, hh).wait_recv()

        def one(i):
            spot = pl.ds(pl.multiple_of((lax.rem(h + 1 + i, line) * 2 + x) * depth, depth), depth)
            weight_terms[c, spot] = (
                weight_terms[c, spot].astype(F32)
                + weight_x[c, lax.rem(h + 1 + i, line)].astype(F32)
            ).astype(BF16)

        repeat(line, one)
        for s in range(1, line):
            g_far(c, s).start()

    def weight_finish(c):
        for s in range(1, line):
            g_far(c, s).wait_recv()
        total = weight_terms[c, times(h * 2 + x, depth)].astype(F32)
        for s in range(1, line):
            total = total + weight_far[c, s - 1].astype(F32)
        weight_out[:, times(c, wide)] = total.astype(BF16)

    def values_part(w, c):
        return jnp.dot(
            window[w * length : (w + 1) * length], full[:, times(c, wide)],
            preferred_element_type=F32,
        )

    def send_part(c):
        part_send[c] = values_part(1, c).astype(BF16)
        part_copy(c).start()

    def keep_part(c):
        near[c] = values_part(0, c)

    tile = 256

    def input_terms(w):
        def one(n):
            left = jnp.concatenate(
                [grads_in[c, w * length : (w + 1) * length] for c in range(chunks)], axis=1
            )
            terms[w * length : (w + 1) * length, times(n, tile)] = lax.dot_general(
                left, full[times(n, tile)], (((1,), (1,)), ((), ())), preferred_element_type=F32
            ).astype(BF16)

        repeat(half // tile, one)
        for i in range(tall):
            t_core(w, i).start()

    strip = 32

    def terms_pass(w):
        for i in range(tall):
            t_core(w, i).wait_recv()

        def one(at):
            i = at // (rows // strip)
            r = lax.rem(at, rows // strip) * strip
            spot = pl.ds(
                pl.multiple_of(w * length + (2 * i + core) * rows + r, strip), strip
            )
            terms[spot] = (
                terms[spot].astype(F32)
                + terms_core[w, i, pl.ds(pl.multiple_of(r, strip), strip)].astype(F32)
            ).astype(BF16)

        repeat(tall * (rows // strip), one)
        for s in range(1, tall):
            t_y(w, s).start()

    def terms_finish(w):
        for s in range(1, tall):
            t_y(w, s).wait_recv()

        def one(at):
            spot = pl.ds(pl.multiple_of(at * strip, strip), strip)
            total = terms[
                pl.ds(pl.multiple_of(w * length + me_ctx * rows + at * strip, strip), strip)
            ].astype(F32)
            for s in range(1, tall):
                total = total + terms_y[w, s - 1, spot].astype(F32)
            result[w, spot] = total.astype(BF16)

        repeat(rows // strip, one)
        for g in range(line):
            (t_z(g) if w == 1 else t_local(g)).start()

    greet(dp, ctx)
    for g in range(line):
        f_local(g).start()
    for g in range(line):
        f_z(g).start()
    gates_start(0)
    for p in range(chunks):
        w_x(p).start()
        for s in range(1, line):
            w_far(s, p).start()
    own_weight.start()
    for g in range(line):
        f_local(g).wait()
    f_core(0, 0).start()
    for s in range(1, tall):
        f_y(0, s).start()
    if chunks > 1:
        gates_start(1)
    streams[:, :8] = jnp.zeros((3, 8, LANES), F32)
    grads[:, length:] = jnp.zeros((3, 8, LANES), F32)
    product[: product.shape[0] - length] = jnp.zeros((product.shape[0] - length, LANES), BF16)
    small[...] = jnp.zeros_like(small)

    lag = 2
    last = chunks - 1

    def early(c):
        for s in range(1, line):
            w_far(s, c).wait_recv()
            w_relay(s, c).start()

        @pl.when(c == 0)
        def _():
            for g in range(line):
                f_z(g).wait_recv()
            f_core(1, 0).start()
            for s in range(1, tall):
                f_y(1, s).start()
            for later in range(2, chunks):
                gates_start(later)

        @pl.when(c == min(1, last))
        def _():
            for s in range(1, tall):
                f_y(0, s).wait_recv()
                f_core(0, s).start()

        @pl.when(c == min(2, last))
        def _():
            for s in range(1, tall):
                f_y(1, s).wait_recv()
                f_core(1, s).start()
            for w in range(2):
                for s in range(tall):
                    f_core(w, s).wait_recv()

        if chunks > lag:

            @pl.when(c >= lag)
            def _():
                weight_term(c - lag)

        gates_wait(c)
        stage_one(c)
        grad_copy(c).start()

    repeat(chunks, early)
    own_weight.wait()
    for p in range(chunks):
        w_x(p).wait_recv()
        for s in range(1, line):
            w_relay(s, p).wait_recv()
    repeat(chunks, send_part)
    rest = max(chunks - lag, 0)
    repeat(chunks - rest, lambda i: weight_term(rest + i))
    input_terms(0)
    weight_pass(0)
    repeat(chunks, keep_part)
    terms_pass(0)
    if chunks > 1:
        weight_pass(1)
    input_terms(1)

    def late(c):
        part_copy(c).wait_recv()
        stage_two(c)

        @pl.when(c == 0)
        def _():
            terms_pass(1)

        @pl.when(c + 2 < chunks)
        def _():
            weight_pass(c + 2)

        @pl.when(c == min(2, last))
        def _():
            terms_finish(1)

    repeat(chunks, late)
    terms_finish(0)
    repeat(chunks, weight_finish)

    def small_wait(c):
        for s in range(1, dp):
            small_copy(c, s).wait_recv()

    repeat(chunks, small_wait)
    edge = short_out.shape[1]
    for c in range(chunks):
        total = small_send[c].astype(F32)
        for s in range(1, dp):
            total = total + small_recv[s - 1, c].astype(F32)
        for index in range(3):
            short_out[index, :, c * wide : (c + 1) * wide] = total[8 * index : 8 * index + edge]
        for u in range(per):
            at = (c * per + u) * groups
            medium_out[at : at + groups] = total[24:32, u * LANES : (u + 1) * LANES]

    for g in range(line):
        t_local(g).wait()
        t_z(g).wait()
        f_z(g).wait_send()
    for w in range(2):
        for s in range(tall):
            f_core(w, s).wait_send()
            t_core(w, s).wait_send()
        for s in range(1, tall):
            f_y(w, s).wait_send()
            t_y(w, s).wait_send()

    def drain(c):
        w_x(c).wait_send()
        for s in range(1, line):
            w_far(s, c).wait_send()
            w_relay(s, c).wait_send()
            g_far(c, s).wait_send()
        for which in range(3):
            for s in range(1, ctx):
                gates(c, which, s).wait_send()
                outs(c, which, s).wait()
            outs_local(c, which).wait()
        grad_copy(c).wait_send()
        part_copy(c).wait_send()
        for hh in range(line):
            g_x(c, hh).wait_send()
        for s in range(1, dp):
            small_copy(c, s).wait_send()

    repeat(chunks, drain)


def fused(
    dp, ctx, group_width, row_scale, group_scale,
    features, gate_in, gate_out, cot, weight, taps, ahead, behind,
):
    rows, channels = features.shape
    depth, cols = weight.shape
    length, edge, span = rows * ctx, taps.shape[1], ahead.shape[1] // 2
    groups = LANES // group_width
    wide = min(256, cols)
    chunks, places = cols // wide, cols // LANES
    plan = Plan(dp, ctx, chunks)
    line, tall = plan.line, plan.tall
    half = 2 * line * depth
    f32, bf16 = (lambda *shape: pltpu.VMEM(shape, F32)), (lambda *shape: pltpu.VMEM(shape, BF16))
    shapes = [(depth, cols)] + [(rows, channels)] * 4
    dma = pltpu.SemaphoreType.DMA
    return pl.pallas_call(
        functools.partial(fused_kernel, plan, group_width, row_scale, group_scale),
        out_shape=[jax.ShapeDtypeStruct(shape, BF16) for shape in shapes]
        + [
            jax.ShapeDtypeStruct((3, edge, cols), F32),
            jax.ShapeDtypeStruct((ahead.shape[0], span), F32),
        ],
        in_specs=[ANY] * 5 + [VMEM] * 3,
        out_specs=[VMEM] * 7,
        scratch_shapes=[
            bf16(2 * length, half), bf16(half, cols), bf16(3, chunks, length, wide),
            bf16(chunks, 2 * length, wide), f32(chunks, length, wide),
            bf16(chunks, length, wide), bf16(chunks, length, wide),
            bf16(2 * length, half), bf16(2, tall, rows, half),
            bf16(2, max(tall - 1, 1), rows, half),
            bf16(chunks, half, wide), bf16(chunks, line, depth, wide),
            bf16(chunks, max(line - 1, 1), depth, wide), bf16(3, chunks, length, wide),
            f32(32, wide), bf16(chunks, 32, wide), bf16(dp - 1, chunks, 32, wide),
            bf16(2, rows, half),
            f32(places, length, LANES), f32(places, length, LANES),
            bf16(places, length + span, LANES), f32(places, length, LANES),
            f32(3, length + 8, LANES), f32(3, length + 8, LANES), bf16(length + span, LANES),
            f32(length, LANES), bf16(groups * span, 2 * span),
            dma((plan.remote,)), dma((plan.remote,)), dma((plan.local,)),
        ],
        compiler_params=pltpu.CompilerParams(
            collective_id=0, has_side_effects=True, vmem_limit_bytes=60 * 2**20
        ),
    )(features, gate_in, gate_out, cot, weight, taps, ahead, behind)


def place_kernel(count, *refs):
    sem = refs[2 * count]
    moves = [
        pltpu.make_async_copy(refs[at], refs[count + at], sem.at[at]) for at in range(count)
    ]
    for move in moves:
        move.start()
    for move in moves:
        move.wait()


def place(arrays):
    count = len(arrays)
    return pl.pallas_call(
        functools.partial(place_kernel, count),
        out_shape=[jax.ShapeDtypeStruct(array.shape, array.dtype) for array in arrays],
        in_specs=[VMEM] * count,
        out_specs=[ANY] * count,
        scratch_shapes=[pltpu.SemaphoreType.DMA((count,))],
    )(*arrays)


def local(features, gate_in, gate_out, value_weight, short_taps, medium_taps, cotangent):
    ctx = lax.axis_size("ctx")
    dp = lax.axis_size("dp")
    ctx_index = lax.axis_index("ctx")
    rows, channels = features.shape
    cols = value_weight.shape[1]
    span, group_count = medium_taps.shape
    group_width = channels // group_count
    total_rows = rows * ctx * dp
    row_scale = 1.0 / math.sqrt(total_rows)
    group_scale = 1.0 / math.sqrt(total_rows * group_width)
    taps = lax.dynamic_slice_in_dim(short_taps, ctx_index * cols, cols, 2)
    own_groups = group_count // ctx
    medium = lax.dynamic_slice_in_dim(medium_taps, ctx_index * own_groups, own_groups, 1)
    lifted = medium.astype(F32).T
    zeros = jnp.zeros((own_groups, span), F32)
    ahead = jnp.concatenate([zeros[:, :1], lifted[:, ::-1], zeros[:, 1:]], axis=1)
    behind = jnp.concatenate([lifted, zeros], axis=1)
    *wide_outs, grad_short, grad_medium = fused(
        dp, ctx, group_width, row_scale, group_scale,
        features, gate_in, gate_out, cotangent, value_weight, taps, ahead, behind,
    )
    weight_out, grad_features, layer_out, first_out, second_out, grad_short = place(
        list(wide_outs) + [grad_short]
    )
    return (
        layer_out,
        grad_features,
        first_out,
        second_out,
        weight_out,
        grad_short,
        grad_medium[:, ::-1].T,
    )


def solution(mesh):
    rows, split = P(("dp", "ctx"), None), P("dp", "ctx")
    return jax.shard_map(
        local,
        mesh=mesh,
        in_specs=(rows, rows, rows, split, P(), P(), rows),
        out_specs=(rows, rows, rows, rows, split, P(None, None, "ctx"), P(None, "ctx")),
        check_vma=False,
    )
```
